32 devices in a mesh: section: 2 (over core), ctx: 4 (over y, x), tp: 4 (over z).
Axes of the slice: x: 2, y: 2, z: 4, core: 2. Of those that a mesh axis runs over, the one named last changes fastest.
Arguments:
- inputs: bfloat16 [2, 2, 1024, 2048], P(None, None, 'ctx'), may hold values from -6 to 6
- grad_out: float32 [2, 2, 1024, 2048], P(None, None, 'ctx'), may hold values from -6 to 6
- ln1_gain: bfloat16 [2, 2048], P('section', 'ctx'), may hold values from 0.5 to 1.5
- ln1_bias: bfloat16 [2, 2048], P('section', 'ctx'), may hold values from -3 to 3
- ln2_gain: bfloat16 [2, 2048], P('section', 'ctx'), may hold values from 0.5 to 1.5
- ln2_bias: bfloat16 [2, 2048], P('section', 'ctx'), may hold values from -3 to 3
- w_qkv: bfloat16 [2, 2048, 8, 768], P('section', 'ctx', 'tp'), may hold values from -0.125 to 0.125
- qkv_bias: bfloat16 [2, 8, 768], P('section', 'tp', 'ctx'), may hold values from -3 to 3
- w_dense: bfloat16 [2, 2048, 2048], P('section', 'tp', 'ctx'), may hold values from -1.5 to 1.5
- w_up: bfloat16 [2, 2048, 8192], P('section', 'ctx', 'tp'), may hold values from -0.125 to 0.125
- up_bias: bfloat16 [2, 8192], P('section', ('tp', 'ctx')), may hold values from -3 to 3
- w_down: bfloat16 [2, 8192, 2048], P('section', 'tp', 'ctx'), may hold values from -0.0625 to 0.0625
- out_bias: bfloat16 [2, 2048], P('section', 'ctx'), may hold values from -3 to 3
Outputs:
- block_ends: float32 [2, 2, 2, 1024, 2048], P('section', None, None, 'ctx')
- grad_ln1_gain: float32 [2, 2048], P('section', 'ctx')
- grad_ln1_bias: float32 [2, 2048], P('section', 'ctx')
- grad_ln2_gain: float32 [2, 2048], P('section', 'ctx')
- grad_ln2_bias: float32 [2, 2048], P('section', 'ctx')
- grad_w_qkv: float32 [2, 2048, 8, 768], P('section', 'ctx', 'tp')
- grad_qkv_bias: float32 [2, 8, 768], P('section', 'tp', 'ctx')
- grad_w_dense: float32 [2, 2048, 2048], P('section', 'tp', 'ctx')
- grad_w_up: float32 [2, 2048, 8192], P('section', 'ctx', 'tp')
- grad_up_bias: float32 [2, 8192], P('section', ('tp', 'ctx'))
- grad_w_down: float32 [2, 8192, 2048], P('section', 'tp', 'ctx')
- grad_out_bias: float32 [2, 2048], P('section', 'ctx')
The draws below stay inside these ranges and needn't reach their ends.
All inputs are finite; a program needn't handle non-finite values.
Results may differ from the reference program's by a relative error of at most 0.022.
Values may be sent and summed in bfloat16 or wider, within the bound.
A program may use at most 384 MiB of HBM per device.

```python
import math
import jax
import jax.numpy as jnp
from jax import lax

D = 2048
H = 8
HD = 256
FF = 8192
ROT = 64
SEQS = 2
MICRO = 2
LAYERS = 2
LEN = 1024
N_SECTION = 2


def block_scale(own_key, extent, pieces, smallest, high):
    def one(position, blocks):
        draws = jax.random.uniform(jax.random.fold_in(jax.random.fold_in(own_key, 6), position), (blocks,), jnp.float32, smallest / len(pieces), high / len(pieces))
        return jnp.repeat(jnp.exp(draws), extent[position] // blocks).reshape((-1,) + (1,) * (len(extent) - position - 1))

    factor_of = one(*pieces[0])
    for cut in pieces[1:]:
        factor_of = factor_of * one(*cut)
    return factor_of


def noise(key, shape, spread, most, shards=(), kind=jnp.bfloat16):
    entries = jax.random.normal(key, shape, jnp.float32) * spread
    if len(shards) > 0:
        entries = block_scale(key, shape, shards, -0.22, 0.18) * entries
    return jnp.clip(entries, min=-most, max=most).astype(kind)


def setup_inputs(seed: int = 0) -> dict:
    key_list = jax.random.split(jax.random.key(seed), 14)
    inputs = noise(key_list[0], (MICRO, SEQS, LEN, D), 1.0, 6.0, ((2, 4),))
    grad_out = noise(key_list[1], (MICRO, SEQS, LEN, D), 1.0, 6.0, ((2, 4),), jnp.float32)
    ln1_gain = jnp.clip(1.0 + 0.1 * jax.random.normal(key_list[2], (LAYERS, D), jnp.float32), 0.5, 1.5).astype(jnp.bfloat16)
    ln1_bias = noise(key_list[3], (LAYERS, D), 0.5, 3.0, ((0, 2), (1, 4)))
    ln2_gain = jnp.clip(1.0 + 0.1 * jax.random.normal(key_list[4], (LAYERS, D), jnp.float32), 0.5, 1.5).astype(jnp.bfloat16)
    ln2_bias = noise(key_list[5], (LAYERS, D), 0.5, 3.0, ((0, 2), (1, 4)))
    w_qkv = noise(key_list[6], (LAYERS, D, H, 3 * HD), D ** -0.5, 0.125, ((0, 2), (1, 4), (2, 4)))
    qkv_bias = noise(key_list[7], (LAYERS, H, 3 * HD), 0.5, 3.0, ((0, 2), (1, 4), (2, 4)))
    w_dense = noise(key_list[8], (LAYERS, D, D), (HD // 16) ** -0.5, 1.5, ((0, 2), (1, 4), (2, 4)))
    w_up = noise(key_list[9], (LAYERS, D, FF), D ** -0.5, 0.125, ((0, 2), (1, 4), (2, 4)))
    up_bias = noise(key_list[10], (LAYERS, FF), 0.5, 3.0, ((0, 2), (1, 16)))
    w_down = noise(key_list[11], (LAYERS, FF, D), FF ** -0.5, 0.0625, ((0, 2), (1, 4), (2, 4)))
    out_bias = noise(key_list[12], (LAYERS, D), 0.5, 3.0, ((0, 2), (1, 4)))
    return dict(inputs=inputs, grad_out=grad_out, ln1_gain=ln1_gain, ln1_bias=ln1_bias, ln2_gain=ln2_gain, ln2_bias=ln2_bias, w_qkv=w_qkv, qkv_bias=qkv_bias, w_dense=w_dense, w_up=w_up, up_bias=up_bias, w_down=w_down, out_bias=out_bias)


norm_eps = 1e-05
root_half = 1.0 / math.sqrt(2.0)
root_tau = 1.0 / math.sqrt(2.0 * math.pi)

def layer_norm(row_block, gain_vec, shift_vec):
    row_mean = lax.optimization_barrier(jnp.mean(row_block, axis=-1, keepdims=True))
    centered = row_block - row_mean
    row_var = lax.optimization_barrier(jnp.mean(centered * centered, axis=-1, keepdims=True))
    inverse = lax.rsqrt(row_var + norm_eps)
    unit_rows = centered * inverse
    return (unit_rows * gain_vec + shift_vec, unit_rows, inverse)

def norm_back(grad_rows, unit_rows, inverse, gain_vec):
    scaled = grad_rows * gain_vec
    first_mean = lax.optimization_barrier(jnp.mean(scaled, axis=-1, keepdims=True))
    second_mean = lax.optimization_barrier(jnp.mean(scaled * unit_rows, axis=-1, keepdims=True))
    return inverse * (scaled - first_mean - unit_rows * second_mean)

def gelu_parts(values):
    normal_cdf = 0.5 * (1.0 + lax.erf(values * root_half))
    return (values * normal_cdf, normal_cdf + values * jnp.exp(-0.5 * values * values) * root_tau)

def rotary_tables(positions, rot_width):
    half_width = rot_width // 2
    frequency = jnp.exp(jnp.arange(half_width).astype(jnp.float32) * (-2.0 * math.log(10000.0) / rot_width))
    angles = positions[:, None] * frequency[None, :]
    cosine = jnp.cos(angles)
    sine = jnp.sin(angles)
    return (jnp.concatenate([cosine, cosine], -1)[:, None, :], jnp.concatenate([sine, sine], -1)[:, None, :])

def rotate_heads(features, cosine, sine):
    rot_width = cosine.shape[-1]
    half_width = rot_width // 2
    rotated_part = features[..., :rot_width]
    turned = jnp.concatenate([-rotated_part[..., half_width:], rotated_part[..., :half_width]], -1)
    return jnp.concatenate([rotated_part * cosine + turned * sine, features[..., rot_width:]], -1)

def rotate_back(grads, cosine, sine):
    rot_width = cosine.shape[-1]
    half_width = rot_width // 2
    rotated_part = grads[..., :rot_width]
    weighted = rotated_part * sine
    turned = jnp.concatenate([weighted[..., half_width:], -weighted[..., :half_width]], -1)
    return jnp.concatenate([rotated_part * cosine + turned, grads[..., rot_width:]], -1)

def dot_transposed(left, right):
    return lax.dot_general(left, right, (((1,), (1,)), ((), ())), preferred_element_type=jnp.float32)

def transposed_dot(left, right):
    return lax.dot_general(left, right, (((0,), (0,)), ((), ())), preferred_element_type=jnp.float32)

def head_forward(query_head, key_head, value_head, allowed, score_scale):
    scores = jnp.where(allowed, dot_transposed(query_head, key_head) * score_scale, -1e+30)
    row_top = lax.optimization_barrier(jnp.max(scores, axis=-1, keepdims=True))
    row_total = lax.optimization_barrier(jnp.sum(jnp.exp(scores - row_top), axis=-1, keepdims=True))
    log_total = row_top + jnp.log(row_total)
    probabilities = jnp.where(allowed, jnp.exp(scores - log_total), 0.0)
    context_head = jnp.dot(probabilities.astype(jnp.bfloat16), value_head, preferred_element_type=jnp.float32).astype(jnp.bfloat16)
    return (context_head, log_total)

def head_backward(query_head, key_head, value_head, context_head, log_total, grad_head, allowed, score_scale):
    scores = jnp.where(allowed, dot_transposed(query_head, key_head) * score_scale, -1e+30)
    probabilities = jnp.where(allowed, jnp.exp(scores - log_total), 0.0)
    grad_half = grad_head.astype(jnp.bfloat16)
    row_delta = lax.optimization_barrier(jnp.sum(grad_head * context_head.astype(jnp.float32), axis=-1, keepdims=True))
    grad_probs = dot_transposed(grad_half, value_head)
    grad_scores = (probabilities * (grad_probs - row_delta)).astype(jnp.bfloat16)
    grad_query = jnp.dot(grad_scores, key_head, preferred_element_type=jnp.float32) * score_scale
    grad_key = transposed_dot(grad_scores, query_head) * score_scale
    grad_value = transposed_dot(probabilities.astype(jnp.bfloat16), grad_half)
    return (grad_query, grad_key, grad_value)

def layer_forward(layer_rows, layer_params, cosine, sine, allowed):
    gain_one, bias_one, gain_two, bias_two, qkv_weight, qkv_shift, dense_weight, up_weight, up_shift, down_weight, out_shift = layer_params
    score_scale = 1.0 / math.sqrt(HD)
    flat_rows = layer_rows.astype(jnp.float32)
    normed_one, unit_one, inverse_one = layer_norm(flat_rows, gain_one.astype(jnp.float32), bias_one.astype(jnp.float32))
    normed_two, unit_two, inverse_two = layer_norm(flat_rows, gain_two.astype(jnp.float32), bias_two.astype(jnp.float32))
    input_one = normed_one.astype(jnp.bfloat16)
    input_two = normed_two.astype(jnp.bfloat16)
    mixed_rows = jnp.dot(input_one, qkv_weight.reshape(D, 3 * D), preferred_element_type=jnp.float32) + qkv_shift.astype(jnp.float32).reshape(3 * D)
    mixed_rows = mixed_rows.reshape(LEN, H, 3 * HD)
    query_rows = rotate_heads(mixed_rows[..., :HD], cosine, sine).astype(jnp.bfloat16)
    key_rows = rotate_heads(mixed_rows[..., HD:2 * HD], cosine, sine).astype(jnp.bfloat16)
    value_rows = mixed_rows[..., 2 * HD:].astype(jnp.bfloat16)
    context, log_total = lax.map(lambda trio: head_forward(trio[0], trio[1], trio[2], allowed, score_scale), (query_rows.transpose(1, 0, 2), key_rows.transpose(1, 0, 2), value_rows.transpose(1, 0, 2)))
    context = context.transpose(1, 0, 2)
    pre_act = jnp.dot(input_two, up_weight, preferred_element_type=jnp.float32) + up_shift.astype(jnp.float32)
    activated, slope = gelu_parts(pre_act)
    active = activated.astype(jnp.bfloat16)
    branch = jnp.dot(context.reshape(LEN, D), dense_weight, preferred_element_type=jnp.float32) + jnp.dot(active, down_weight, preferred_element_type=jnp.float32)
    result = flat_rows + branch + out_shift.astype(jnp.float32)
    saved_state = (unit_one, inverse_one, unit_two, inverse_two, input_one, input_two, query_rows, key_rows, value_rows, context, log_total, slope, active)
    return (result, saved_state)

def layer_backward(layer_rows, grad_rows, layer_params, cosine, sine, allowed):
    gain_one, bias_one, gain_two, bias_two, qkv_weight, qkv_shift, dense_weight, up_weight, up_shift, down_weight, out_shift = layer_params
    score_scale = 1.0 / math.sqrt(HD)
    result, saved_state = layer_forward(layer_rows, layer_params, cosine, sine, allowed)
    unit_one, inverse_one, unit_two, inverse_two, input_one, input_two, query_rows, key_rows, value_rows, context, log_total, slope, active = saved_state
    grad_half = grad_rows.astype(jnp.bfloat16)
    grad_out_shift = lax.optimization_barrier(jnp.sum(grad_rows, 0))
    grad_down = transposed_dot(active, grad_half)
    grad_pre = dot_transposed(grad_half, down_weight) * slope
    grad_up_shift = lax.optimization_barrier(jnp.sum(grad_pre, 0))
    pre_half = grad_pre.astype(jnp.bfloat16)
    grad_up = transposed_dot(input_two, pre_half)
    back_two = dot_transposed(pre_half, up_weight)
    grad_dense = transposed_dot(context.reshape(LEN, D), grad_half)
    grad_context = dot_transposed(grad_half, dense_weight).reshape(LEN, H, HD)
    grad_query, grad_key, grad_value = lax.map(lambda group: head_backward(group[0], group[1], group[2], group[3], group[4], group[5], allowed, score_scale), (query_rows.transpose(1, 0, 2), key_rows.transpose(1, 0, 2), value_rows.transpose(1, 0, 2), context.transpose(1, 0, 2), log_total, grad_context.transpose(1, 0, 2)))
    grad_mixed = jnp.concatenate([rotate_back(grad_query.transpose(1, 0, 2), cosine, sine), rotate_back(grad_key.transpose(1, 0, 2), cosine, sine), grad_value.transpose(1, 0, 2)], -1)
    grad_qkv_shift = lax.optimization_barrier(jnp.sum(grad_mixed, 0))
    mixed_half = grad_mixed.reshape(LEN, 3 * D).astype(jnp.bfloat16)
    grad_qkv = transposed_dot(input_one, mixed_half).reshape(D, H, 3 * HD)
    back_one = dot_transposed(mixed_half, qkv_weight.reshape(D, 3 * D))
    grad_gain_one = lax.optimization_barrier(jnp.sum(back_one * unit_one, 0))
    grad_bias_one = lax.optimization_barrier(jnp.sum(back_one, 0))
    grad_gain_two = lax.optimization_barrier(jnp.sum(back_two * unit_two, 0))
    grad_bias_two = lax.optimization_barrier(jnp.sum(back_two, 0))
    grad_input = grad_rows + norm_back(back_one, unit_one, inverse_one, gain_one.astype(jnp.float32)) + norm_back(back_two, unit_two, inverse_two, gain_two.astype(jnp.float32))
    return (grad_input, (grad_gain_one, grad_bias_one, grad_gain_two, grad_bias_two, grad_qkv, grad_qkv_shift, grad_dense, grad_up, grad_up_shift, grad_down, grad_out_shift))

def reference(inputs, grad_out, ln1_gain, ln1_bias, ln2_gain, ln2_bias, w_qkv, qkv_bias, w_dense, w_up, up_bias, w_down, out_bias):
    weight_list = (ln1_gain, ln1_bias, ln2_gain, ln2_bias, w_qkv, qkv_bias, w_dense, w_up, up_bias, w_down, out_bias)
    position_index = jnp.arange(LEN).astype(jnp.int32)
    allowed = position_index[None, :] <= position_index[:, None]
    cosine, sine = rotary_tables(position_index.astype(jnp.float32), ROT)
    layer_rows = inputs.reshape(MICRO * SEQS, LEN, D)
    layer_inputs = []
    for layer_index in range(N_SECTION):
        layer_params = tuple((weight[layer_index] for weight in weight_list))
        layer_inputs.append(layer_rows)
        result = lax.map(lambda seq_rows: layer_forward(seq_rows, layer_params, cosine, sine, allowed)[0], layer_rows)
        if layer_index + 1 < N_SECTION:
            layer_rows = result.astype(jnp.bfloat16)
        else:
            layer_rows = result
    final_rows = layer_rows
    grad_rows = grad_out.reshape(MICRO * SEQS, LEN, D).astype(jnp.float32)
    layer_grads = [None] * N_SECTION
    for layer_index in reversed(range(N_SECTION)):
        layer_params = tuple((weight[layer_index] for weight in weight_list))
        zero_totals = tuple((jnp.zeros(weight.shape[1:], jnp.float32) for weight in weight_list))

        def add_sequence(totals, seq_pair):
            grad_back, grad_terms = layer_backward(seq_pair[0], seq_pair[1], layer_params, cosine, sine, allowed)
            return (tuple((left + right for left, right in zip(totals, grad_terms))), grad_back)
        totals, grad_rows = lax.scan(add_sequence, zero_totals, (layer_inputs[layer_index], grad_rows))
        layer_grads[layer_index] = totals
    stacked = [jnp.stack([layer_grads[layer_index][entry] for layer_index in range(N_SECTION)]) for entry in range(11)]
    block_ends = jnp.stack([grad_rows, final_rows]).reshape(2, MICRO, SEQS, LEN, D)
    return (block_ends, stacked[0], stacked[1], stacked[2], stacked[3], stacked[4], stacked[5], stacked[6], stacked[7], stacked[8], stacked[9], stacked[10])
```

```python
import math

import jax
import jax.numpy as jnp
from jax import lax
from jax.sharding import PartitionSpec as P

norm_eps = 1e-05
root_half = 1.0 / math.sqrt(2.0)
root_tau = 1.0 / math.sqrt(2.0 * math.pi)


def one_way(value, src, dst):
    return lax.ppermute(value, "section", [(src, dst)])


def swap_sections(value):
    return lax.ppermute(value, "section", [(0, 1), (1, 0)])


def gelu_parts(values):
    normal_cdf = 0.5 * (1.0 + lax.erf(values * root_half))
    return (values * normal_cdf, normal_cdf + values * jnp.exp(-0.5 * values * values) * root_tau)


def rotary_tables(positions, rot_width):
    half_width = rot_width // 2
    frequency = jnp.exp(
        jnp.arange(half_width).astype(jnp.float32) * (-2.0 * math.log(10000.0) / rot_width)
    )
    angles = positions[:, None] * frequency[None, :]
    cosine = jnp.cos(angles)
    sine = jnp.sin(angles)
    return (
        jnp.concatenate([cosine, cosine], -1)[:, None, :],
        jnp.concatenate([sine, sine], -1)[:, None, :],
    )


def rotate_heads(features, cosine, sine):
    rot_width = cosine.shape[-1]
    half_width = rot_width // 2
    rotated_part = features[..., :rot_width]
    turned = jnp.concatenate([-rotated_part[..., half_width:], rotated_part[..., :half_width]], -1)
    return jnp.concatenate([rotated_part * cosine + turned * sine, features[..., rot_width:]], -1)


def rotate_back(grads, cosine, sine):
    rot_width = cosine.shape[-1]
    half_width = rot_width // 2
    rotated_part = grads[..., :rot_width]
    weighted = rotated_part * sine
    turned = jnp.concatenate([weighted[..., half_width:], -weighted[..., :half_width]], -1)
    return jnp.concatenate([rotated_part * cosine + turned, grads[..., rot_width:]], -1)


def dot_transposed(left, right):
    return lax.dot_general(
        left, right, (((1,), (1,)), ((), ())), preferred_element_type=jnp.float32
    )


def transposed_dot(left, right):
    return lax.dot_general(
        left, right, (((0,), (0,)), ((), ())), preferred_element_type=jnp.float32
    )


def masked_scores(query_rows, key_all, allowed, score_scale):
    scores = (
        jnp.einsum("sqhd,skhd->shqk", query_rows, key_all, preferred_element_type=jnp.float32)
        * score_scale
    )
    return jnp.where(allowed, scores, -1e30)


def attend_heads(query_rows, key_all, value_all, allowed, score_scale):
    scores = masked_scores(query_rows, key_all, allowed, score_scale)
    row_top = jnp.max(scores, axis=-1, keepdims=True)
    row_total = jnp.sum(jnp.exp(scores - row_top), axis=-1, keepdims=True)
    log_total = row_top + jnp.log(row_total)
    probabilities = jnp.where(allowed, jnp.exp(scores - log_total), 0.0)
    context = jnp.einsum(
        "shqk,skhd->sqhd",
        probabilities.astype(jnp.bfloat16),
        value_all,
        preferred_element_type=jnp.float32,
    ).astype(jnp.bfloat16)
    return (context, log_total)


def attend_back(
    query_rows, key_all, value_all, context, log_total, grad_context, allowed, score_scale
):
    scores = masked_scores(query_rows, key_all, allowed, score_scale)
    probabilities = jnp.where(allowed, jnp.exp(scores - log_total), 0.0)
    grad_half = grad_context.astype(jnp.bfloat16)
    row_delta = jnp.sum(grad_context * context.astype(jnp.float32), axis=-1).transpose(0, 2, 1)[
        ..., None
    ]
    grad_probs = jnp.einsum(
        "sqhd,skhd->shqk", grad_half, value_all, preferred_element_type=jnp.float32
    )
    grad_scores = (probabilities * (grad_probs - row_delta)).astype(jnp.bfloat16)
    grad_query = (
        jnp.einsum("shqk,skhd->sqhd", grad_scores, key_all, preferred_element_type=jnp.float32)
        * score_scale
    )
    grad_key = (
        jnp.einsum("shqk,sqhd->skhd", grad_scores, query_rows, preferred_element_type=jnp.float32)
        * score_scale
    )
    grad_value = jnp.einsum(
        "shqk,sqhd->skhd",
        probabilities.astype(jnp.bfloat16),
        grad_half,
        preferred_element_type=jnp.float32,
    )
    return (grad_query, grad_key, grad_value)


def gather_layer(ln1_gain, ln1_bias, ln2_gain, ln2_bias, w_qkv, qkv_bias, w_dense, w_up,
                 up_bias, w_down, out_bias):
    gains = lax.all_gather(
        jnp.concatenate([ln1_gain, ln1_bias, ln2_gain, ln2_bias, out_bias], 0),
        "ctx", axis=1, tiled=True,
    )
    return (
        gains,
        lax.all_gather(up_bias[0], "ctx", axis=0, tiled=True),
        lax.all_gather(w_qkv[0], "ctx", axis=0, tiled=True),
        lax.all_gather(qkv_bias[0], "ctx", axis=1, tiled=True),
        lax.all_gather(w_dense[0], "ctx", axis=1, tiled=True),
        lax.all_gather(w_up[0], "ctx", axis=0, tiled=True),
        lax.all_gather(w_down[0], "ctx", axis=1, tiled=True),
    )


def layer_forward(rows, weights, cosine, sine, allowed, score_scale):
    gains, up_shift, qkv_full, qkv_shift, dense_full, up_full, down_full = weights
    seq_count, tok_rows, model_width = rows.shape
    head_count = qkv_full.shape[1]
    head_dim = qkv_full.shape[2] // 3
    flat_count = seq_count * tok_rows
    gain_one, bias_one, gain_two, bias_two, out_shift = (
        gains[i].astype(jnp.float32) for i in range(5)
    )
    up_shift = up_shift.astype(jnp.float32)
    flat_rows = rows.reshape(flat_count, model_width).astype(jnp.float32)
    row_mean = jnp.mean(flat_rows, axis=-1, keepdims=True)
    centered = flat_rows - row_mean
    row_var = jnp.mean(centered * centered, axis=-1, keepdims=True)
    inverse = lax.rsqrt(row_var + norm_eps)
    unit = centered * inverse
    input_one = (unit * gain_one + bias_one).astype(jnp.bfloat16)
    input_two = (unit * gain_two + bias_two).astype(jnp.bfloat16)
    mixed_rows = jnp.dot(
        input_one, qkv_full.reshape(model_width, -1), preferred_element_type=jnp.float32
    ) + qkv_shift.astype(jnp.float32).reshape(-1)
    mixed_rows = mixed_rows.reshape(seq_count, tok_rows, head_count, 3 * head_dim)
    query_rows = rotate_heads(mixed_rows[..., :head_dim], cosine, sine).astype(jnp.bfloat16)
    key_rows = rotate_heads(mixed_rows[..., head_dim : 2 * head_dim], cosine, sine).astype(
        jnp.bfloat16
    )
    value_rows = mixed_rows[..., 2 * head_dim :].astype(jnp.bfloat16)
    key_all = lax.all_gather(key_rows, "ctx", axis=1, tiled=True)
    value_all = lax.all_gather(value_rows, "ctx", axis=1, tiled=True)
    context, log_total = attend_heads(query_rows, key_all, value_all, allowed, score_scale)
    pre_act = jnp.dot(input_two, up_full, preferred_element_type=jnp.float32) + up_shift
    activated, slope = gelu_parts(pre_act)
    active = activated.astype(jnp.bfloat16)
    partial_sum = jnp.dot(
        context.reshape(flat_count, -1), dense_full, preferred_element_type=jnp.float32
    )
    partial_sum = partial_sum + jnp.dot(active, down_full, preferred_element_type=jnp.float32)
    branch = lax.psum(partial_sum.astype(jnp.bfloat16), "tp").astype(jnp.float32)
    result = (flat_rows + branch + out_shift).reshape(seq_count, tok_rows, model_width)
    saved = (unit, inverse, input_one, input_two, query_rows, key_all, value_all, context,
             log_total, slope, active)
    return result, saved


def layer_backward(grad_rows, saved, weights, cosine, sine, allowed, score_scale):
    gains, _, qkv_full, qkv_shift, dense_full, up_full, down_full = weights
    (unit, inverse, input_one, input_two, query_rows, key_all, value_all, context, log_total,
     slope, active) = saved
    seq_count, tok_rows, model_width = grad_rows.shape
    head_count = qkv_full.shape[1]
    head_dim = qkv_full.shape[2] // 3
    flat_count = seq_count * tok_rows
    gain_one = gains[0].astype(jnp.float32)
    gain_two = gains[2].astype(jnp.float32)
    grad_flat = grad_rows.reshape(flat_count, model_width)
    grad_half = grad_flat.astype(jnp.bfloat16)
    grad_out_shift = jnp.sum(grad_flat, 0)
    grad_down = transposed_dot(active, grad_half)
    grad_pre = dot_transposed(grad_half, down_full) * slope
    grad_up_shift = jnp.sum(grad_pre, 0)
    pre_half = grad_pre.astype(jnp.bfloat16)
    grad_up = transposed_dot(input_two, pre_half)
    back_two = dot_transposed(pre_half, up_full)
    grad_dense = transposed_dot(context.reshape(flat_count, -1), grad_half)
    grad_context = dot_transposed(grad_half, dense_full).reshape(
        seq_count, tok_rows, head_count, head_dim
    )
    grad_query, grad_key_all, grad_value_all = attend_back(
        query_rows, key_all, value_all, context, log_total, grad_context, allowed, score_scale
    )
    key_value_grads = lax.psum_scatter(
        jnp.stack([grad_key_all, grad_value_all]).astype(jnp.bfloat16),
        "ctx",
        scatter_dimension=2,
        tiled=True,
    ).astype(jnp.float32)
    grad_mixed = jnp.concatenate(
        [
            rotate_back(grad_query, cosine, sine),
            rotate_back(key_value_grads[0], cosine, sine),
            key_value_grads[1],
        ],
        -1,
    )
    grad_qkv_shift = jnp.sum(grad_mixed, (0, 1))
    mixed_half = grad_mixed.reshape(flat_count, -1).astype(jnp.bfloat16)
    grad_qkv = transposed_dot(input_one, mixed_half).reshape(qkv_full.shape)
    back_one = dot_transposed(mixed_half, qkv_full.reshape(model_width, -1))
    norm_terms = jnp.stack(
        [
            jnp.sum(back_one * unit, 0),
            jnp.sum(back_one, 0),
            jnp.sum(back_two * unit, 0),
            jnp.sum(back_two, 0),
        ]
    )
    scaled = lax.psum(
        (back_one * gain_one + back_two * gain_two).astype(jnp.bfloat16), "tp"
    ).astype(jnp.float32)
    first_mean = jnp.mean(scaled, axis=-1, keepdims=True)
    second_mean = jnp.mean(scaled * unit, axis=-1, keepdims=True)
    grad_input = grad_flat + inverse * (scaled - first_mean - unit * second_mean)
    small = jnp.concatenate(
        [norm_terms, grad_out_shift[None]], 0
    )
    grad_terms = (small, grad_qkv, grad_qkv_shift, grad_dense, grad_up, grad_up_shift, grad_down)
    return grad_input.reshape(seq_count, tok_rows, model_width), grad_terms


def on_device(
    inputs,
    grad_out,
    ln1_gain,
    ln1_bias,
    ln2_gain,
    ln2_bias,
    w_qkv,
    qkv_bias,
    w_dense,
    w_up,
    up_bias,
    w_down,
    out_bias,
):
    section_index = lax.axis_index("section")
    context_index = lax.axis_index("ctx")
    ctx_count = lax.axis_size("ctx")
    micro_count, seq_count, tok_rows, model_width = inputs.shape
    seq_length = tok_rows * ctx_count
    head_dim = w_qkv.shape[3] // 3
    score_scale = 1.0 / math.sqrt(head_dim)

    own = gather_layer(ln1_gain, ln1_bias, ln2_gain, ln2_bias, w_qkv, qkv_bias, w_dense, w_up,
                       up_bias, w_down, out_bias)
    other = tuple(swap_sections(piece) for piece in own)
    first_layer = tuple(jnp.where(section_index == 0, a, b) for a, b in zip(own, other))
    second_layer = tuple(jnp.where(section_index == 0, b, a) for a, b in zip(own, other))

    query_index = context_index * tok_rows + jnp.arange(tok_rows, dtype=jnp.int32)
    allowed = jnp.arange(seq_length, dtype=jnp.int32)[None, :] <= query_index[:, None]
    cosine, sine = rotary_tables(query_index.astype(jnp.float32), head_dim // 4)

    rows = jnp.where(section_index == 0, inputs[0], inputs[1])
    grads = jnp.where(section_index == 0, grad_out[0], grad_out[1])

    mid, saved_first = layer_forward(rows, first_layer, cosine, sine, allowed, score_scale)
    top, saved_second = layer_forward(
        mid.astype(jnp.bfloat16), second_layer, cosine, sine, allowed, score_scale
    )
    top_other = one_way(top, 0, 1)

    grad_mid, terms_second = layer_backward(
        grads, saved_second, second_layer, cosine, sine, allowed, score_scale
    )
    second_other = tuple(one_way(t.astype(jnp.bfloat16), 0, 1) for t in terms_second)
    grad_in, terms_first = layer_backward(
        grad_mid, saved_first, first_layer, cosine, sine, allowed, score_scale
    )
    first_other = tuple(one_way(t.astype(jnp.bfloat16), 1, 0) for t in terms_first)
    grad_other = one_way(grad_in, 1, 0)

    totals = tuple(
        jnp.where(
            section_index == 0,
            a + b.astype(jnp.float32),
            c + d.astype(jnp.float32),
        )
        for a, b, c, d in zip(terms_first, first_other, terms_second, second_other)
    )
    small, g_qkv, g_qkv_shift, g_dense, g_up, g_up_shift, g_down = totals
    small = lax.psum(small[:4], "tp")
    small = jnp.concatenate([small, totals[0][4:]], 0)

    def scatter(value, axis):
        return lax.psum_scatter(
            value.astype(jnp.bfloat16), "ctx", scatter_dimension=axis, tiled=True
        ).astype(jnp.float32)

    small = scatter(small, 1)
    g_qkv = scatter(g_qkv, 0)
    g_qkv_shift = scatter(g_qkv_shift, 1)
    g_dense = scatter(g_dense, 1)
    g_up = scatter(g_up, 0)
    g_up_shift = scatter(g_up_shift, 0)
    g_down = scatter(g_down, 1)

    block_ends = jnp.where(
        section_index == 0,
        jnp.stack([grad_in, grad_other]),
        jnp.stack([top_other, top]),
    )[None]
    return (
        block_ends,
        small[0][None],
        small[1][None],
        small[2][None],
        small[3][None],
        g_qkv[None],
        g_qkv_shift[None],
        g_dense[None],
        g_up[None],
        g_up_shift[None],
        g_down[None],
        small[4][None],
    )


def solution(mesh):
    placed = (
        P(None, None, "ctx", None),
        P(None, None, "ctx", None),
        P("section", "ctx"),
        P("section", "ctx"),
        P("section", "ctx"),
        P("section", "ctx"),
        P("section", "ctx", "tp", None),
        P("section", "tp", "ctx"),
        P("section", "tp", "ctx"),
        P("section", "ctx", "tp"),
        P("section", ("tp", "ctx")),
        P("section", "tp", "ctx"),
        P("section", "ctx"),
    )
    return jax.shard_map(
        on_device,
        mesh=mesh,
        in_specs=placed,
        out_specs=(
            P("section", None, None, "ctx", None),
            P("section", "ctx"),
            P("section", "ctx"),
            P("section", "ctx"),
            P("section", "ctx"),
            P("section", "ctx", "tp", None),
            P("section", "tp", "ctx"),
            P("section", "tp", "ctx"),
            P("section", "ctx", "tp"),
            P("section", ("tp", "ctx")),
            P("section", "tp", "ctx"),
            P("section", "ctx"),
        ),
        check_vma=False,
    )
```

```python
import math

import jax
import jax.numpy as jnp
from jax import lax
from jax.sharding import PartitionSpec as P

norm_eps = 1e-05
root_half = 1.0 / math.sqrt(2.0)
root_tau = 1.0 / math.sqrt(2.0 * math.pi)


def one_way(value, src, dst):
    return lax.ppermute(value, "section", [(src, dst)])


def swap_sections(value):
    return lax.ppermute(value, "section", [(0, 1), (1, 0)])


def causal_gather(block, axis):
    count = lax.axis_size("ctx")
    index = lax.axis_index("ctx")
    width = block.shape[axis]
    shape = list(block.shape)
    shape[axis] = count * width
    full = jnp.zeros(shape, block.dtype)
    for shift in range(count - 1, 0, -1):
        moved = lax.ppermute(block, "ctx", [(i, i + shift) for i in range(count - shift)])
        full = lax.dynamic_update_slice_in_dim(full, moved, (index - shift) * width, axis)
    return lax.dynamic_update_slice_in_dim(full, block, index * width, axis)


def causal_return(full, axis):
    count = lax.axis_size("ctx")
    index = lax.axis_index("ctx")
    width = full.shape[axis] // count
    total = lax.dynamic_slice_in_dim(full, index * width, width, axis)
    for shift in range(1, count):
        piece = lax.dynamic_slice_in_dim(full, (index - shift) * width, width, axis)
        moved = lax.ppermute(
            piece.astype(jnp.bfloat16), "ctx", [(i + shift, i) for i in range(count - shift)]
        )
        total = total + moved.astype(jnp.float32)
    return total


def gelu_parts(values):
    normal_cdf = 0.5 * (1.0 + lax.erf(values * root_half))
    return (values * normal_cdf, normal_cdf + values * jnp.exp(-0.5 * values * values) * root_tau)


def rotary_tables(positions, rot_width):
    half_width = rot_width // 2
    frequency = jnp.exp(
        jnp.arange(half_width).astype(jnp.float32) * (-2.0 * math.log(10000.0) / rot_width)
    )
    angles = positions[:, None] * frequency[None, :]
    cosine = jnp.cos(angles)
    sine = jnp.sin(angles)
    return (
        jnp.concatenate([cosine, cosine], -1)[:, None, :],
        jnp.concatenate([sine, sine], -1)[:, None, :],
    )


def rotate_heads(features, cosine, sine):
    rot_width = cosine.shape[-1]
    half_width = rot_width // 2
    rotated_part = features[..., :rot_width]
    turned = jnp.concatenate([-rotated_part[..., half_width:], rotated_part[..., :half_width]], -1)
    return jnp.concatenate([rotated_part * cosine + turned * sine, features[..., rot_width:]], -1)


def rotate_back(grads, cosine, sine):
    rot_width = cosine.shape[-1]
    half_width = rot_width // 2
    rotated_part = grads[..., :rot_width]
    weighted = rotated_part * sine
    turned = jnp.concatenate([weighted[..., half_width:], -weighted[..., :half_width]], -1)
    return jnp.concatenate([rotated_part * cosine + turned, grads[..., rot_width:]], -1)


def dot_transposed(left, right):
    return lax.dot_general(
        left, right, (((1,), (1,)), ((), ())), preferred_element_type=jnp.float32
    )


def transposed_dot(left, right):
    return lax.dot_general(
        left, right, (((0,), (0,)), ((), ())), preferred_element_type=jnp.float32
    )


def masked_scores(query_rows, key_all, allowed, score_scale):
    scores = (
        jnp.einsum("sqhd,skhd->shqk", query_rows, key_all, preferred_element_type=jnp.float32)
        * score_scale
    )
    return jnp.where(allowed, scores, -1e30)


def attend_heads(query_rows, key_all, value_all, allowed, score_scale):
    scores = masked_scores(query_rows, key_all, allowed, score_scale)
    row_top = jnp.max(scores, axis=-1, keepdims=True)
    row_total = jnp.sum(jnp.exp(scores - row_top), axis=-1, keepdims=True)
    log_total = row_top + jnp.log(row_total)
    probabilities = jnp.where(allowed, jnp.exp(scores - log_total), 0.0)
    context = jnp.einsum(
        "shqk,skhd->sqhd",
        probabilities.astype(jnp.bfloat16),
        value_all,
        preferred_element_type=jnp.float32,
    ).astype(jnp.bfloat16)
    return (context, log_total)


def attend_back(
    query_rows, key_all, value_all, context, log_total, grad_context, allowed, score_scale
):
    scores = masked_scores(query_rows, key_all, allowed, score_scale)
    probabilities = jnp.where(allowed, jnp.exp(scores - log_total), 0.0)
    grad_half = grad_context.astype(jnp.bfloat16)
    row_delta = jnp.sum(grad_context * context.astype(jnp.float32), axis=-1).transpose(0, 2, 1)[
        ..., None
    ]
    grad_probs = jnp.einsum(
        "sqhd,skhd->shqk", grad_half, value_all, preferred_element_type=jnp.float32
    )
    grad_scores = (probabilities * (grad_probs - row_delta)).astype(jnp.bfloat16)
    grad_query = (
        jnp.einsum("shqk,skhd->sqhd", grad_scores, key_all, preferred_element_type=jnp.float32)
        * score_scale
    )
    grad_key = (
        jnp.einsum("shqk,sqhd->skhd", grad_scores, query_rows, preferred_element_type=jnp.float32)
        * score_scale
    )
    grad_value = jnp.einsum(
        "shqk,sqhd->skhd",
        probabilities.astype(jnp.bfloat16),
        grad_half,
        preferred_element_type=jnp.float32,
    )
    return (grad_query, grad_key, grad_value)


def gather_layer(ln1_gain, ln1_bias, ln2_gain, ln2_bias, w_qkv, qkv_bias, w_dense, w_up,
                 up_bias, w_down, out_bias):
    gains = lax.all_gather(
        jnp.concatenate([ln1_gain, ln1_bias, ln2_gain, ln2_bias, out_bias], 0),
        "ctx", axis=1, tiled=True,
    )
    return (
        gains,
        lax.all_gather(up_bias[0], "ctx", axis=0, tiled=True),
        lax.all_gather(w_qkv[0], "ctx", axis=0, tiled=True),
        lax.all_gather(qkv_bias[0], "ctx", axis=1, tiled=True),
        lax.all_gather(w_dense[0], "ctx", axis=1, tiled=True),
        lax.all_gather(w_up[0], "ctx", axis=0, tiled=True),
        lax.all_gather(w_down[0], "ctx", axis=1, tiled=True),
    )


def layer_forward(rows, weights, cosine, sine, allowed, score_scale):
    gains, up_shift, qkv_full, qkv_shift, dense_full, up_full, down_full = weights
    seq_count, tok_rows, model_width = rows.shape
    head_count = qkv_full.shape[1]
    head_dim = qkv_full.shape[2] // 3
    flat_count = seq_count * tok_rows
    gain_one, bias_one, gain_two, bias_two, out_shift = (
        gains[i].astype(jnp.float32) for i in range(5)
    )
    up_shift = up_shift.astype(jnp.float32)
    flat_rows = rows.reshape(flat_count, model_width).astype(jnp.float32)
    row_mean = jnp.mean(flat_rows, axis=-1, keepdims=True)
    centered = flat_rows - row_mean
    row_var = jnp.mean(centered * centered, axis=-1, keepdims=True)
    inverse = lax.rsqrt(row_var + norm_eps)
    unit = centered * inverse
    input_one = (unit * gain_one + bias_one).astype(jnp.bfloat16)
    input_two = (unit * gain_two + bias_two).astype(jnp.bfloat16)
    mixed_rows = jnp.dot(
        input_one, qkv_full.reshape(model_width, -1), preferred_element_type=jnp.float32
    ) + qkv_shift.astype(jnp.float32).reshape(-1)
    mixed_rows = mixed_rows.reshape(seq_count, tok_rows, head_count, 3 * head_dim)
    query_rows = rotate_heads(mixed_rows[..., :head_dim], cosine, sine).astype(jnp.bfloat16)
    key_rows = rotate_heads(mixed_rows[..., head_dim : 2 * head_dim], cosine, sine).astype(
        jnp.bfloat16
    )
    value_rows = mixed_rows[..., 2 * head_dim :].astype(jnp.bfloat16)
    key_all, value_all = causal_gather(jnp.stack([key_rows, value_rows]), 2)
    context, log_total = attend_heads(query_rows, key_all, value_all, allowed, score_scale)
    pre_act = jnp.dot(input_two, up_full, preferred_element_type=jnp.float32) + up_shift
    activated, slope = gelu_parts(pre_act)
    active = activated.astype(jnp.bfloat16)
    partial_sum = jnp.dot(
        context.reshape(flat_count, -1), dense_full, preferred_element_type=jnp.float32
    )
    partial_sum = partial_sum + jnp.dot(active, down_full, preferred_element_type=jnp.float32)
    branch = lax.psum(partial_sum.astype(jnp.bfloat16), "tp").astype(jnp.float32)
    result = (flat_rows + branch + out_shift).reshape(seq_count, tok_rows, model_width)
    saved = (unit, inverse, input_one, input_two, query_rows, key_all, value_all, context,
             log_total, slope, active)
    return result, saved


def layer_backward(grad_rows, saved, weights, cosine, sine, allowed, score_scale, tie):
    gains, _, qkv_full, qkv_shift, dense_full, up_full, down_full = weights
    (unit, inverse, input_one, input_two, query_rows, key_all, value_all, context, log_total,
     slope, active) = saved
    seq_count, tok_rows, model_width = grad_rows.shape
    head_count = qkv_full.shape[1]
    head_dim = qkv_full.shape[2] // 3
    flat_count = seq_count * tok_rows
    gain_one = gains[0].astype(jnp.float32)
    gain_two = gains[2].astype(jnp.float32)
    grad_flat = grad_rows.reshape(flat_count, model_width)
    grad_half = grad_flat.astype(jnp.bfloat16)
    grad_out_shift = jnp.sum(grad_flat, 0)
    grad_down = transposed_dot(active, grad_half)
    grad_pre = dot_transposed(grad_half, down_full) * slope
    grad_up_shift = jnp.sum(grad_pre, 0)
    pre_half = grad_pre.astype(jnp.bfloat16)
    grad_up = transposed_dot(input_two, pre_half)
    back_two = dot_transposed(pre_half, up_full)
    grad_dense = transposed_dot(context.reshape(flat_count, -1), grad_half)
    grad_context = dot_transposed(grad_half, dense_full).reshape(
        seq_count, tok_rows, head_count, head_dim
    )
    grad_query, grad_key_all, grad_value_all = attend_back(
        query_rows, key_all, value_all, context, log_total, grad_context, allowed, score_scale
    )
    key_value_grads = causal_return(jnp.stack([grad_key_all, grad_value_all]), 2)
    grad_mixed = jnp.concatenate(
        [
            rotate_back(grad_query, cosine, sine),
            rotate_back(key_value_grads[0], cosine, sine),
            key_value_grads[1],
        ],
        -1,
    )
    grad_qkv_shift = jnp.sum(grad_mixed, (0, 1))
    mixed_half = grad_mixed.reshape(flat_count, -1).astype(jnp.bfloat16)
    grad_qkv = transposed_dot(input_one, mixed_half).reshape(qkv_full.shape)
    back_one = dot_transposed(mixed_half, qkv_full.reshape(model_width, -1))
    norm_terms = jnp.stack(
        [
            jnp.sum(back_one * unit, 0),
            jnp.sum(back_one, 0),
            jnp.sum(back_two * unit, 0),
            jnp.sum(back_two, 0),
        ]
    )
    scaled = (back_one * gain_one + back_two * gain_two).astype(jnp.bfloat16)
    tie, scaled = lax.optimization_barrier((tie, scaled))
    scaled = lax.psum(scaled, "tp").astype(jnp.float32)
    first_mean = jnp.mean(scaled, axis=-1, keepdims=True)
    second_mean = jnp.mean(scaled * unit, axis=-1, keepdims=True)
    grad_input = grad_flat + inverse * (scaled - first_mean - unit * second_mean)
    small = jnp.concatenate(
        [norm_terms, grad_out_shift[None]], 0
    )
    grad_terms = (small, grad_qkv, grad_qkv_shift, grad_dense, grad_up, grad_up_shift, grad_down)
    return grad_input.reshape(seq_count, tok_rows, model_width), grad_terms, tie


SPLIT_AXES = (None, 2, None, 0, 1, None, 0)
CTX_AXES = (1, 0, 1, 1, 0, 0, 1)


def reduce_layer(terms, owner):
    section_index = lax.axis_index("section")
    ctx_count = lax.axis_size("ctx")
    context_index = lax.axis_index("ctx")
    small = terms[0]
    small = jnp.concatenate([lax.psum(small[:4], "tp"), small[4:]], 0)
    tiny = [small, terms[2], terms[5]]
    tiny_axes = [1, 1, 0]
    flat = []
    sizes = []
    for value, axis in zip(tiny, tiny_axes):
        moved = jnp.moveaxis(value, axis, 0)
        sizes.append(moved.shape)
        flat.append(moved.reshape(ctx_count, -1))
    packed = lax.psum(jnp.concatenate(flat, 1), ("section", "ctx"))
    packed = lax.dynamic_index_in_dim(packed, context_index, 0, keepdims=False)
    pieces = []
    offset = 0
    for shape, axis in zip(sizes, tiny_axes):
        width = math.prod(shape) // ctx_count
        piece = packed[offset : offset + width].reshape((shape[0] // ctx_count,) + shape[1:])
        pieces.append(jnp.moveaxis(piece, 0, axis))
        offset += width
    out = [pieces[0], None, pieces[1], None, None, pieces[2], None]
    for position in (1, 3, 4, 6):
        value = terms[position]
        split_axis = SPLIT_AXES[position]
        half = value.shape[split_axis] // 2
        mine = lax.dynamic_slice_in_dim(value, section_index * half, half, split_axis)
        theirs = lax.dynamic_slice_in_dim(value, (1 - section_index) * half, half, split_axis)
        summed = mine + swap_sections(theirs.astype(jnp.bfloat16)).astype(jnp.float32)
        reduced = lax.psum_scatter(
            summed.astype(jnp.bfloat16), "ctx", scatter_dimension=CTX_AXES[position], tiled=True
        ).astype(jnp.float32)
        moved = one_way(reduced, 1 - owner, owner)
        halves = [reduced, moved] if owner == 0 else [moved, reduced]
        out[position] = jnp.concatenate(halves, split_axis)
    return tuple(out)


def on_device(
    inputs,
    grad_out,
    ln1_gain,
    ln1_bias,
    ln2_gain,
    ln2_bias,
    w_qkv,
    qkv_bias,
    w_dense,
    w_up,
    up_bias,
    w_down,
    out_bias,
):
    section_index = lax.axis_index("section")
    context_index = lax.axis_index("ctx")
    ctx_count = lax.axis_size("ctx")
    micro_count, seq_count, tok_rows, model_width = inputs.shape
    seq_length = tok_rows * ctx_count
    head_dim = w_qkv.shape[3] // 3
    score_scale = 1.0 / math.sqrt(head_dim)

    own = gather_layer(ln1_gain, ln1_bias, ln2_gain, ln2_bias, w_qkv, qkv_bias, w_dense, w_up,
                       up_bias, w_down, out_bias)
    other = tuple(swap_sections(piece) for piece in own)
    first_layer = tuple(jnp.where(section_index == 0, a, b) for a, b in zip(own, other))
    second_layer = tuple(jnp.where(section_index == 0, b, a) for a, b in zip(own, other))

    query_index = context_index * tok_rows + jnp.arange(tok_rows, dtype=jnp.int32)
    allowed = jnp.arange(seq_length, dtype=jnp.int32)[None, :] <= query_index[:, None]
    cosine, sine = rotary_tables(query_index.astype(jnp.float32), head_dim // 4)

    rows = jnp.where(section_index == 0, inputs[0], inputs[1])
    grads = jnp.where(section_index == 0, grad_out[0], grad_out[1])

    mid, saved_first = layer_forward(rows, first_layer, cosine, sine, allowed, score_scale)
    top, saved_second = layer_forward(
        mid.astype(jnp.bfloat16), second_layer, cosine, sine, allowed, score_scale
    )
    grad_mid, terms_second, top = layer_backward(
        grads, saved_second, second_layer, cosine, sine, allowed, score_scale, top
    )
    top_other = one_way(top, 0, 1)
    reduced_second = reduce_layer(terms_second, 1)
    grad_in, terms_first, _ = layer_backward(
        grad_mid, saved_first, first_layer, cosine, sine, allowed, score_scale, grad_mid
    )
    reduced_first = reduce_layer(terms_first, 0)
    grad_other = one_way(grad_in, 1, 0)
    small, g_qkv, g_qkv_shift, g_dense, g_up, g_up_shift, g_down = (
        jnp.where(section_index == 0, a, b) for a, b in zip(reduced_first, reduced_second)
    )

    block_ends = jnp.where(
        section_index == 0,
        jnp.stack([grad_in, grad_other]),
        jnp.stack([top_other, top]),
    )[None]
    return (
        block_ends,
        small[0][None],
        small[1][None],
        small[2][None],
        small[3][None],
        g_qkv[None],
        g_qkv_shift[None],
        g_dense[None],
        g_up[None],
        g_up_shift[None],
        g_down[None],
        small[4][None],
    )


def solution(mesh):
    placed = (
        P(None, None, "ctx", None),
        P(None, None, "ctx", None),
        P("section", "ctx"),
        P("section", "ctx"),
        P("section", "ctx"),
        P("section", "ctx"),
        P("section", "ctx", "tp", None),
        P("section", "tp", "ctx"),
        P("section", "tp", "ctx"),
        P("section", "ctx", "tp"),
        P("section", ("tp", "ctx")),
        P("section", "tp", "ctx"),
        P("section", "ctx"),
    )
    return jax.shard_map(
        on_device,
        mesh=mesh,
        in_specs=placed,
        out_specs=(
            P("section", None, None, "ctx", None),
            P("section", "ctx"),
            P("section", "ctx"),
            P("section", "ctx"),
            P("section", "ctx"),
            P("section", "ctx", "tp", None),
            P("section", "tp", "ctx"),
            P("section", "tp", "ctx"),
            P("section", "ctx", "tp"),
            P("section", ("tp", "ctx")),
            P("section", "tp", "ctx"),
            P("section", "ctx"),
        ),
        check_vma=False,
    )
```

```python
import math

import jax
import jax.numpy as jnp
from jax import lax
from jax.sharding import PartitionSpec as P

norm_eps = 1e-05
root_half = 1.0 / math.sqrt(2.0)
root_tau = 1.0 / math.sqrt(2.0 * math.pi)


def one_way(value, src, dst):
    return lax.ppermute(value, "section", [(src, dst)])


def swap_sections(value):
    return lax.ppermute(value, "section", [(0, 1), (1, 0)])


def causal_gather(block, axis):
    count = lax.axis_size("ctx")
    index = lax.axis_index("ctx")
    width = block.shape[axis]
    shape = list(block.shape)
    shape[axis] = count * width
    full = jnp.zeros(shape, block.dtype)
    for shift in range(count - 1, 0, -1):
        moved = lax.ppermute(block, "ctx", [(i, i + shift) for i in range(count - shift)])
        full = lax.dynamic_update_slice_in_dim(full, moved, (index - shift) * width, axis)
    return lax.dynamic_update_slice_in_dim(full, block, index * width, axis)


def causal_return(full, axis):
    count = lax.axis_size("ctx")
    index = lax.axis_index("ctx")
    width = full.shape[axis] // count
    total = lax.dynamic_slice_in_dim(full, index * width, width, axis)
    for shift in range(1, count):
        piece = lax.dynamic_slice_in_dim(full, (index - shift) * width, width, axis)
        moved = lax.ppermute(
            piece.astype(jnp.bfloat16), "ctx", [(i + shift, i) for i in range(count - shift)]
        )
        total = total + moved.astype(jnp.float32)
    return total


def gelu_parts(values):
    normal_cdf = 0.5 * (1.0 + lax.erf(values * root_half))
    return (values * normal_cdf, normal_cdf + values * jnp.exp(-0.5 * values * values) * root_tau)


def rotary_tables(positions, rot_width):
    half_width = rot_width // 2
    frequency = jnp.exp(
        jnp.arange(half_width).astype(jnp.float32) * (-2.0 * math.log(10000.0) / rot_width)
    )
    angles = positions[:, None] * frequency[None, :]
    cosine = jnp.cos(angles)
    sine = jnp.sin(angles)
    return (
        jnp.concatenate([cosine, cosine], -1)[:, None, :],
        jnp.concatenate([sine, sine], -1)[:, None, :],
    )


def rotate_heads(features, cosine, sine):
    rot_width = cosine.shape[-1]
    half_width = rot_width // 2
    rotated_part = features[..., :rot_width]
    turned = jnp.concatenate([-rotated_part[..., half_width:], rotated_part[..., :half_width]], -1)
    return jnp.concatenate([rotated_part * cosine + turned * sine, features[..., rot_width:]], -1)


def rotate_back(grads, cosine, sine):
    rot_width = cosine.shape[-1]
    half_width = rot_width // 2
    rotated_part = grads[..., :rot_width]
    weighted = rotated_part * sine
    turned = jnp.concatenate([weighted[..., half_width:], -weighted[..., :half_width]], -1)
    return jnp.concatenate([rotated_part * cosine + turned, grads[..., rot_width:]], -1)


def dot_transposed(left, right):
    return lax.dot_general(
        left, right, (((1,), (1,)), ((), ())), preferred_element_type=jnp.float32
    )


def transposed_dot(left, right):
    return lax.dot_general(
        left, right, (((0,), (0,)), ((), ())), preferred_element_type=jnp.float32
    )


def masked_scores(query_rows, key_all, allowed, score_scale):
    scores = (
        jnp.einsum("sqhd,skhd->shqk", query_rows, key_all, preferred_element_type=jnp.float32)
        * score_scale
    )
    return jnp.where(allowed, scores, -1e30)


def attend_heads(query_rows, key_all, value_all, allowed, score_scale):
    scores = masked_scores(query_rows, key_all, allowed, score_scale)
    row_top = jnp.max(scores, axis=-1, keepdims=True)
    row_total = jnp.sum(jnp.exp(scores - row_top), axis=-1, keepdims=True)
    log_total = row_top + jnp.log(row_total)
    probabilities = jnp.where(allowed, jnp.exp(scores - log_total), 0.0)
    context = jnp.einsum(
        "shqk,skhd->sqhd",
        probabilities.astype(jnp.bfloat16),
        value_all,
        preferred_element_type=jnp.float32,
    ).astype(jnp.bfloat16)
    return (context, log_total)


def attend_back(
    query_rows, key_all, value_all, context, log_total, grad_context, allowed, score_scale
):
    scores = masked_scores(query_rows, key_all, allowed, score_scale)
    probabilities = jnp.where(allowed, jnp.exp(scores - log_total), 0.0)
    grad_half = grad_context.astype(jnp.bfloat16)
    row_delta = jnp.sum(grad_context * context.astype(jnp.float32), axis=-1).transpose(0, 2, 1)[
        ..., None
    ]
    grad_probs = jnp.einsum(
        "sqhd,skhd->shqk", grad_half, value_all, preferred_element_type=jnp.float32
    )
    grad_scores = (probabilities * (grad_probs - row_delta)).astype(jnp.bfloat16)
    grad_query = (
        jnp.einsum("shqk,skhd->sqhd", grad_scores, key_all, preferred_element_type=jnp.float32)
        * score_scale
    )
    grad_key = (
        jnp.einsum("shqk,sqhd->skhd", grad_scores, query_rows, preferred_element_type=jnp.float32)
        * score_scale
    )
    grad_value = jnp.einsum(
        "shqk,sqhd->skhd",
        probabilities.astype(jnp.bfloat16),
        grad_half,
        preferred_element_type=jnp.float32,
    )
    return (grad_query, grad_key, grad_value)


def section_pairs(owner, shift):
    count = lax.axis_size("ctx")
    return [(owner * count + i, owner * count + (i + shift) % count) for i in range(count)]


def owner_gather(shard, owner, axis):
    count = lax.axis_size("ctx")
    index = lax.axis_index("ctx")
    width = shard.shape[axis]
    shape = list(shard.shape)
    shape[axis] = count * width
    full = lax.dynamic_update_slice_in_dim(jnp.zeros(shape, shard.dtype), shard, index * width, axis)
    for shift in range(1, count):
        moved = lax.ppermute(shard, ("section", "ctx"), section_pairs(owner, shift))
        full = lax.dynamic_update_slice_in_dim(
            full, moved, lax.rem(index - shift + count, count) * width, axis
        )
    return full


def owner_scatter(total, owner, axis):
    count = lax.axis_size("ctx")
    index = lax.axis_index("ctx")
    width = total.shape[axis] // count
    result = lax.dynamic_slice_in_dim(total, index * width, width, axis)
    for shift in range(1, count):
        piece = lax.dynamic_slice_in_dim(
            total, lax.rem(index + shift, count) * width, width, axis
        )
        moved = lax.ppermute(
            piece.astype(jnp.bfloat16), ("section", "ctx"), section_pairs(owner, shift)
        )
        result = result + moved.astype(jnp.float32)
    return result


def layer_weights(params, owner):
    (ln1_gain, ln1_bias, ln2_gain, ln2_bias, w_qkv, qkv_bias, w_dense, w_up, up_bias, w_down,
     out_bias) = params
    section_index = lax.axis_index("section")
    count = lax.axis_size("ctx")
    gains = jnp.concatenate([ln1_gain, ln1_bias, ln2_gain, ln2_bias, out_bias], 0)
    packed = jnp.concatenate(
        [gains.reshape(-1), up_bias.reshape(-1), qkv_bias.reshape(-1)]
    )[None]
    packed = owner_gather(packed, owner, 0)
    gain_size = gains.size
    bias_size = up_bias.size
    gains_full = packed[:, :gain_size].reshape(count, 5, -1).transpose(1, 0, 2).reshape(5, -1)
    up_full_shift = packed[:, gain_size : gain_size + bias_size].reshape(-1)
    qkv_shift = packed[:, gain_size + bias_size :].reshape((count,) + qkv_bias.shape[1:])
    qkv_shift = qkv_shift.transpose(1, 0, 2).reshape(qkv_bias.shape[1], -1)
    pieces = (
        gains_full,
        up_full_shift,
        owner_gather(w_qkv[0], owner, 0),
        qkv_shift,
        owner_gather(w_dense[0], owner, 1),
        owner_gather(w_up[0], owner, 0),
        owner_gather(w_down[0], owner, 1),
    )
    return tuple(
        jnp.where(section_index == owner, piece, one_way(piece, owner, 1 - owner))
        for piece in pieces
    )


def reduce_layer(terms, owner):
    section_index = lax.axis_index("section")
    ctx_count = lax.axis_size("ctx")
    context_index = lax.axis_index("ctx")
    small = terms[0]
    small = jnp.concatenate([lax.psum(small[:4], "tp"), small[4:]], 0)
    tiny = [small, terms[2], terms[5]]
    tiny_axes = [1, 1, 0]
    flat = []
    sizes = []
    for value, axis in zip(tiny, tiny_axes):
        moved = jnp.moveaxis(value, axis, 0)
        sizes.append(moved.shape)
        flat.append(moved.reshape(ctx_count, -1))
    packed = lax.psum(jnp.concatenate(flat, 1), ("section", "ctx"))
    packed = lax.dynamic_index_in_dim(packed, context_index, 0, keepdims=False)
    pieces = []
    offset = 0
    for shape, axis in zip(sizes, tiny_axes):
        width = math.prod(shape) // ctx_count
        piece = packed[offset : offset + width].reshape((shape[0] // ctx_count,) + shape[1:])
        pieces.append(jnp.moveaxis(piece, 0, axis))
        offset += width
    out = [pieces[0], None, pieces[1], None, None, pieces[2], None]
    for position, axis in ((6, 1), (4, 0), (3, 1), (1, 0)):
        value = terms[position]
        total = value + one_way(value.astype(jnp.bfloat16), 1 - owner, owner).astype(jnp.float32)
        out[position] = owner_scatter(total, owner, axis)
    return tuple(out)


def layer_forward(rows, weights, cosine, sine, allowed, score_scale):
    gains, up_shift, qkv_full, qkv_shift, dense_full, up_full, down_full = weights
    seq_count, tok_rows, model_width = rows.shape
    head_count = qkv_full.shape[1]
    head_dim = qkv_full.shape[2] // 3
    flat_count = seq_count * tok_rows
    gain_one, bias_one, gain_two, bias_two, out_shift = (
        gains[i].astype(jnp.float32) for i in range(5)
    )
    up_shift = up_shift.astype(jnp.float32)
    flat_rows = rows.reshape(flat_count, model_width).astype(jnp.float32)
    row_mean = jnp.mean(flat_rows, axis=-1, keepdims=True)
    centered = flat_rows - row_mean
    row_var = jnp.mean(centered * centered, axis=-1, keepdims=True)
    inverse = lax.rsqrt(row_var + norm_eps)
    unit = centered * inverse
    input_one = (unit * gain_one + bias_one).astype(jnp.bfloat16)
    input_two = (unit * gain_two + bias_two).astype(jnp.bfloat16)
    mixed_rows = jnp.dot(
        input_one, qkv_full.reshape(model_width, -1), preferred_element_type=jnp.float32
    ) + qkv_shift.astype(jnp.float32).reshape(-1)
    mixed_rows = mixed_rows.reshape(seq_count, tok_rows, head_count, 3 * head_dim)
    query_rows = rotate_heads(mixed_rows[..., :head_dim], cosine, sine).astype(jnp.bfloat16)
    key_rows = rotate_heads(mixed_rows[..., head_dim : 2 * head_dim], cosine, sine).astype(
        jnp.bfloat16
    )
    value_rows = mixed_rows[..., 2 * head_dim :].astype(jnp.bfloat16)
    key_all, value_all = causal_gather(jnp.stack([key_rows, value_rows]), 2)
    context, log_total = attend_heads(query_rows, key_all, value_all, allowed, score_scale)
    pre_act = jnp.dot(input_two, up_full, preferred_element_type=jnp.float32) + up_shift
    activated, slope = gelu_parts(pre_act)
    active = activated.astype(jnp.bfloat16)
    partial_sum = jnp.dot(
        context.reshape(flat_count, -1), dense_full, preferred_element_type=jnp.float32
    )
    partial_sum = partial_sum + jnp.dot(active, down_full, preferred_element_type=jnp.float32)
    branch = lax.psum(partial_sum.astype(jnp.bfloat16), "tp").astype(jnp.float32)
    result = (flat_rows + branch + out_shift).reshape(seq_count, tok_rows, model_width)
    saved = (unit, inverse, input_one, input_two, query_rows, key_all, value_all, context,
             log_total, slope, active)
    return result, saved


def layer_backward(grad_rows, saved, weights, cosine, sine, allowed, score_scale, tie):
    gains, _, qkv_full, qkv_shift, dense_full, up_full, down_full = weights
    (unit, inverse, input_one, input_two, query_rows, key_all, value_all, context, log_total,
     slope, active) = saved
    seq_count, tok_rows, model_width = grad_rows.shape
    head_count = qkv_full.shape[1]
    head_dim = qkv_full.shape[2] // 3
    flat_count = seq_count * tok_rows
    gain_one = gains[0].astype(jnp.float32)
    gain_two = gains[2].astype(jnp.float32)
    grad_flat = grad_rows.reshape(flat_count, model_width)
    grad_half = grad_flat.astype(jnp.bfloat16)
    grad_out_shift = jnp.sum(grad_flat, 0)
    grad_down = transposed_dot(active, grad_half)
    grad_pre = dot_transposed(grad_half, down_full) * slope
    grad_up_shift = jnp.sum(grad_pre, 0)
    pre_half = grad_pre.astype(jnp.bfloat16)
    grad_up = transposed_dot(input_two, pre_half)
    back_two = dot_transposed(pre_half, up_full)
    grad_dense = transposed_dot(context.reshape(flat_count, -1), grad_half)
    grad_context = dot_transposed(grad_half, dense_full).reshape(
        seq_count, tok_rows, head_count, head_dim
    )
    grad_query, grad_key_all, grad_value_all = attend_back(
        query_rows, key_all, value_all, context, log_total, grad_context, allowed, score_scale
    )
    key_value_grads = causal_return(jnp.stack([grad_key_all, grad_value_all]), 2)
    grad_mixed = jnp.concatenate(
        [
            rotate_back(grad_query, cosine, sine),
            rotate_back(key_value_grads[0], cosine, sine),
            key_value_grads[1],
        ],
        -1,
    )
    grad_qkv_shift = jnp.sum(grad_mixed, (0, 1))
    mixed_half = grad_mixed.reshape(flat_count, -1).astype(jnp.bfloat16)
    grad_qkv = transposed_dot(input_one, mixed_half).reshape(qkv_full.shape)
    back_one = dot_transposed(mixed_half, qkv_full.reshape(model_width, -1))
    norm_terms = jnp.stack(
        [
            jnp.sum(back_one * unit, 0),
            jnp.sum(back_one, 0),
            jnp.sum(back_two * unit, 0),
            jnp.sum(back_two, 0),
        ]
    )
    scaled = (back_one * gain_one + back_two * gain_two).astype(jnp.bfloat16)
    tie, scaled = lax.optimization_barrier((tie, scaled))
    scaled = lax.psum(scaled, "tp").astype(jnp.float32)
    first_mean = jnp.mean(scaled, axis=-1, keepdims=True)
    second_mean = jnp.mean(scaled * unit, axis=-1, keepdims=True)
    grad_input = grad_flat + inverse * (scaled - first_mean - unit * second_mean)
    small = jnp.concatenate(
        [norm_terms, grad_out_shift[None]], 0
    )
    grad_terms = (small, grad_qkv, grad_qkv_shift, grad_dense, grad_up, grad_up_shift, grad_down)
    return grad_input.reshape(seq_count, tok_rows, model_width), grad_terms, tie


def on_device(
    inputs,
    grad_out,
    ln1_gain,
    ln1_bias,
    ln2_gain,
    ln2_bias,
    w_qkv,
    qkv_bias,
    w_dense,
    w_up,
    up_bias,
    w_down,
    out_bias,
):
    section_index = lax.axis_index("section")
    context_index = lax.axis_index("ctx")
    ctx_count = lax.axis_size("ctx")
    micro_count, seq_count, tok_rows, model_width = inputs.shape
    seq_length = tok_rows * ctx_count
    head_dim = w_qkv.shape[3] // 3
    score_scale = 1.0 / math.sqrt(head_dim)

    params = (ln1_gain, ln1_bias, ln2_gain, ln2_bias, w_qkv, qkv_bias, w_dense, w_up, up_bias,
              w_down, out_bias)
    first_layer = layer_weights(params, 0)
    second_layer = layer_weights(params, 1)

    query_index = context_index * tok_rows + jnp.arange(tok_rows, dtype=jnp.int32)
    allowed = jnp.arange(seq_length, dtype=jnp.int32)[None, :] <= query_index[:, None]
    cosine, sine = rotary_tables(query_index.astype(jnp.float32), head_dim // 4)

    rows = jnp.where(section_index == 0, inputs[0], inputs[1])
    grads = jnp.where(section_index == 0, grad_out[0], grad_out[1])

    mid, saved_first = layer_forward(rows, first_layer, cosine, sine, allowed, score_scale)
    top, saved_second = layer_forward(
        mid.astype(jnp.bfloat16), second_layer, cosine, sine, allowed, score_scale
    )
    grad_mid, terms_second, top = layer_backward(
        grads, saved_second, second_layer, cosine, sine, allowed, score_scale, top
    )
    top_other = one_way(top, 0, 1)
    reduced_second = reduce_layer(terms_second, 1)
    grad_in, terms_first, _ = layer_backward(
        grad_mid, saved_first, first_layer, cosine, sine, allowed, score_scale, grad_mid
    )
    reduced_first = reduce_layer(terms_first, 0)
    grad_other = one_way(grad_in, 1, 0)
    small, g_qkv, g_qkv_shift, g_dense, g_up, g_up_shift, g_down = (
        jnp.where(section_index == 0, a, b) for a, b in zip(reduced_first, reduced_second)
    )

    block_ends = jnp.where(
        section_index == 0,
        jnp.stack([grad_in, grad_other]),
        jnp.stack([top_other, top]),
    )[None]
    return (
        block_ends,
        small[0][None],
        small[1][None],
        small[2][None],
        small[3][None],
        g_qkv[None],
        g_qkv_shift[None],
        g_dense[None],
        g_up[None],
        g_up_shift[None],
        g_down[None],
        small[4][None],
    )


def solution(mesh):
    placed = (
        P(None, None, "ctx", None),
        P(None, None, "ctx", None),
        P("section", "ctx"),
        P("section", "ctx"),
        P("section", "ctx"),
        P("section", "ctx"),
        P("section", "ctx", "tp", None),
        P("section", "tp", "ctx"),
        P("section", "tp", "ctx"),
        P("section", "ctx", "tp"),
        P("section", ("tp", "ctx")),
        P("section", "tp", "ctx"),
        P("section", "ctx"),
    )
    return jax.shard_map(
        on_device,
        mesh=mesh,
        in_specs=placed,
        out_specs=(
            P("section", None, None, "ctx", None),
            P("section", "ctx"),
            P("section", "ctx"),
            P("section", "ctx"),
            P("section", "ctx"),
            P("section", "ctx", "tp", None),
            P("section", "tp", "ctx"),
            P("section", "tp", "ctx"),
            P("section", "ctx", "tp"),
            P("section", ("tp", "ctx")),
            P("section", "tp", "ctx"),
            P("section", "ctx"),
        ),
        check_vma=False,
    )
```

```python
import math

import jax
import jax.numpy as jnp
from jax import lax
from jax.sharding import PartitionSpec as P

norm_eps = 1e-05
root_half = 1.0 / math.sqrt(2.0)
root_tau = 1.0 / math.sqrt(2.0 * math.pi)


def one_way(value, src, dst):
    return lax.ppermute(value, "section", [(src, dst)])


def swap_sections(value):
    return lax.ppermute(value, "section", [(0, 1), (1, 0)])


def causal_gather(block, axis):
    count = lax.axis_size("ctx")
    index = lax.axis_index("ctx")
    width = block.shape[axis]
    shape = list(block.shape)
    shape[axis] = count * width
    full = jnp.zeros(shape, block.dtype)
    for shift in range(count - 1, 0, -1):
        moved = lax.ppermute(block, "ctx", [(i, i + shift) for i in range(count - shift)])
        full = lax.dynamic_update_slice_in_dim(full, moved, (index - shift) * width, axis)
    return lax.dynamic_update_slice_in_dim(full, block, index * width, axis)


def causal_return(full, axis):
    count = lax.axis_size("ctx")
    index = lax.axis_index("ctx")
    width = full.shape[axis] // count
    total = lax.dynamic_slice_in_dim(full, index * width, width, axis)
    for shift in range(1, count):
        piece = lax.dynamic_slice_in_dim(full, (index - shift) * width, width, axis)
        moved = lax.ppermute(
            piece.astype(jnp.bfloat16), "ctx", [(i + shift, i) for i in range(count - shift)]
        )
        total = total + moved.astype(jnp.float32)
    return total


def gelu_parts(values):
    normal_cdf = 0.5 * (1.0 + lax.erf(values * root_half))
    return (values * normal_cdf, normal_cdf + values * jnp.exp(-0.5 * values * values) * root_tau)


def rotary_tables(positions, rot_width):
    half_width = rot_width // 2
    frequency = jnp.exp(
        jnp.arange(half_width).astype(jnp.float32) * (-2.0 * math.log(10000.0) / rot_width)
    )
    angles = positions[:, None] * frequency[None, :]
    cosine = jnp.cos(angles)
    sine = jnp.sin(angles)
    return (
        jnp.concatenate([cosine, cosine], -1)[:, None, :],
        jnp.concatenate([sine, sine], -1)[:, None, :],
    )


def rotate_heads(features, cosine, sine):
    rot_width = cosine.shape[-1]
    half_width = rot_width // 2
    rotated_part = features[..., :rot_width]
    turned = jnp.concatenate([-rotated_part[..., half_width:], rotated_part[..., :half_width]], -1)
    return jnp.concatenate([rotated_part * cosine + turned * sine, features[..., rot_width:]], -1)


def rotate_back(grads, cosine, sine):
    rot_width = cosine.shape[-1]
    half_width = rot_width // 2
    rotated_part = grads[..., :rot_width]
    weighted = rotated_part * sine
    turned = jnp.concatenate([weighted[..., half_width:], -weighted[..., :half_width]], -1)
    return jnp.concatenate([rotated_part * cosine + turned, grads[..., rot_width:]], -1)


def dot_transposed(left, right):
    return lax.dot_general(
        left, right, (((1,), (1,)), ((), ())), preferred_element_type=jnp.float32
    )


def transposed_dot(left, right):
    return lax.dot_general(
        left, right, (((0,), (0,)), ((), ())), preferred_element_type=jnp.float32
    )


def masked_scores(query_rows, key_all, allowed, score_scale):
    scores = (
        jnp.einsum("sqhd,skhd->shqk", query_rows, key_all, preferred_element_type=jnp.float32)
        * score_scale
    )
    return jnp.where(allowed, scores, -1e30)


def attend_heads(query_rows, key_all, value_all, allowed, score_scale):
    scores = masked_scores(query_rows, key_all, allowed, score_scale)
    row_top = jnp.max(scores, axis=-1, keepdims=True)
    row_total = jnp.sum(jnp.exp(scores - row_top), axis=-1, keepdims=True)
    log_total = row_top + jnp.log(row_total)
    probabilities = jnp.where(allowed, jnp.exp(scores - log_total), 0.0)
    context = jnp.einsum(
        "shqk,skhd->sqhd",
        probabilities.astype(jnp.bfloat16),
        value_all,
        preferred_element_type=jnp.float32,
    ).astype(jnp.bfloat16)
    return (context, log_total)


def attend_back(
    query_rows, key_all, value_all, context, log_total, grad_context, allowed, score_scale
):
    scores = masked_scores(query_rows, key_all, allowed, score_scale)
    probabilities = jnp.where(allowed, jnp.exp(scores - log_total), 0.0)
    grad_half = grad_context.astype(jnp.bfloat16)
    row_delta = jnp.sum(grad_context * context.astype(jnp.float32), axis=-1).transpose(0, 2, 1)[
        ..., None
    ]
    grad_probs = jnp.einsum(
        "sqhd,skhd->shqk", grad_half, value_all, preferred_element_type=jnp.float32
    )
    grad_scores = (probabilities * (grad_probs - row_delta)).astype(jnp.bfloat16)
    grad_query = (
        jnp.einsum("shqk,skhd->sqhd", grad_scores, key_all, preferred_element_type=jnp.float32)
        * score_scale
    )
    grad_key = (
        jnp.einsum("shqk,sqhd->skhd", grad_scores, query_rows, preferred_element_type=jnp.float32)
        * score_scale
    )
    grad_value = jnp.einsum(
        "shqk,sqhd->skhd",
        probabilities.astype(jnp.bfloat16),
        grad_half,
        preferred_element_type=jnp.float32,
    )
    return (grad_query, grad_key, grad_value)


def gather_layer(ln1_gain, ln1_bias, ln2_gain, ln2_bias, w_qkv, qkv_bias, w_dense, w_up,
                 up_bias, w_down, out_bias):
    gains = lax.all_gather(
        jnp.concatenate([ln1_gain, ln1_bias, ln2_gain, ln2_bias, out_bias], 0),
        "ctx", axis=1, tiled=True,
    )
    return (
        gains,
        lax.all_gather(up_bias[0], "ctx", axis=0, tiled=True),
        lax.all_gather(w_qkv[0], "ctx", axis=0, tiled=True),
        lax.all_gather(qkv_bias[0], "ctx", axis=1, tiled=True),
        lax.all_gather(w_dense[0], "ctx", axis=1, tiled=True),
        lax.all_gather(w_up[0], "ctx", axis=0, tiled=True),
        lax.all_gather(w_down[0], "ctx", axis=1, tiled=True),
    )


def layer_forward(rows, weights, cosine, sine, allowed, score_scale):
    gains, up_shift, qkv_full, qkv_shift, dense_full, up_full, down_full = weights
    seq_count, tok_rows, model_width = rows.shape
    head_count = qkv_full.shape[1]
    head_dim = qkv_full.shape[2] // 3
    flat_count = seq_count * tok_rows
    gain_one, bias_one, gain_two, bias_two, out_shift = (
        gains[i].astype(jnp.float32) for i in range(5)
    )
    up_shift = up_shift.astype(jnp.float32)
    flat_rows = rows.reshape(flat_count, model_width).astype(jnp.float32)
    row_mean = jnp.mean(flat_rows, axis=-1, keepdims=True)
    centered = flat_rows - row_mean
    row_var = jnp.mean(centered * centered, axis=-1, keepdims=True)
    inverse = lax.rsqrt(row_var + norm_eps)
    unit = centered * inverse
    input_one = (unit * gain_one + bias_one).astype(jnp.bfloat16)
    input_two = (unit * gain_two + bias_two).astype(jnp.bfloat16)
    mixed_rows = jnp.dot(
        input_one, qkv_full.reshape(model_width, -1), preferred_element_type=jnp.float32
    ) + qkv_shift.astype(jnp.float32).reshape(-1)
    mixed_rows = mixed_rows.reshape(seq_count, tok_rows, head_count, 3 * head_dim)
    query_rows = rotate_heads(mixed_rows[..., :head_dim], cosine, sine).astype(jnp.bfloat16)
    key_rows = rotate_heads(mixed_rows[..., head_dim : 2 * head_dim], cosine, sine).astype(
        jnp.bfloat16
    )
    value_rows = mixed_rows[..., 2 * head_dim :].astype(jnp.bfloat16)
    key_all, value_all = causal_gather(jnp.stack([key_rows, value_rows]), 2)
    context, log_total = attend_heads(query_rows, key_all, value_all, allowed, score_scale)
    pre_act = jnp.dot(input_two, up_full, preferred_element_type=jnp.float32) + up_shift
    activated, slope = gelu_parts(pre_act)
    active = activated.astype(jnp.bfloat16)
    partial_sum = jnp.dot(
        context.reshape(flat_count, -1), dense_full, preferred_element_type=jnp.float32
    )
    partial_sum = partial_sum + jnp.dot(active, down_full, preferred_element_type=jnp.float32)
    branch = lax.psum(partial_sum.astype(jnp.bfloat16), "tp").astype(jnp.float32)
    result = (flat_rows + branch + out_shift).reshape(seq_count, tok_rows, model_width)
    saved = (unit, inverse, input_one, input_two, query_rows, key_all, value_all, context,
             log_total, slope, active)
    return result, saved


def layer_backward(grad_rows, saved, weights, cosine, sine, allowed, score_scale, tie):
    gains, _, qkv_full, qkv_shift, dense_full, up_full, down_full = weights
    (unit, inverse, input_one, input_two, query_rows, key_all, value_all, context, log_total,
     slope, active) = saved
    seq_count, tok_rows, model_width = grad_rows.shape
    head_count = qkv_full.shape[1]
    head_dim = qkv_full.shape[2] // 3
    flat_count = seq_count * tok_rows
    gain_one = gains[0].astype(jnp.float32)
    gain_two = gains[2].astype(jnp.float32)
    grad_flat = grad_rows.reshape(flat_count, model_width)
    grad_half = grad_flat.astype(jnp.bfloat16)
    grad_out_shift = jnp.sum(grad_flat, 0)
    grad_down = transposed_dot(active, grad_half)
    grad_pre = dot_transposed(grad_half, down_full) * slope
    grad_up_shift = jnp.sum(grad_pre, 0)
    pre_half = grad_pre.astype(jnp.bfloat16)
    grad_up = transposed_dot(input_two, pre_half)
    back_two = dot_transposed(pre_half, up_full)
    grad_dense = transposed_dot(context.reshape(flat_count, -1), grad_half)
    grad_context = dot_transposed(grad_half, dense_full).reshape(
        seq_count, tok_rows, head_count, head_dim
    )
    grad_query, grad_key_all, grad_value_all = attend_back(
        query_rows, key_all, value_all, context, log_total, grad_context, allowed, score_scale
    )
    key_value_grads = causal_return(jnp.stack([grad_key_all, grad_value_all]), 2)
    grad_mixed = jnp.concatenate(
        [
            rotate_back(grad_query, cosine, sine),
            rotate_back(key_value_grads[0], cosine, sine),
            key_value_grads[1],
        ],
        -1,
    )
    grad_qkv_shift = jnp.sum(grad_mixed, (0, 1))
    mixed_half = grad_mixed.reshape(flat_count, -1).astype(jnp.bfloat16)
    grad_qkv = transposed_dot(input_one, mixed_half).reshape(qkv_full.shape)
    back_one = dot_transposed(mixed_half, qkv_full.reshape(model_width, -1))
    norm_terms = jnp.stack(
        [
            jnp.sum(back_one * unit, 0),
            jnp.sum(back_one, 0),
            jnp.sum(back_two * unit, 0),
            jnp.sum(back_two, 0),
        ]
    )
    scaled = (back_one * gain_one + back_two * gain_two).astype(jnp.bfloat16)
    tie, scaled = lax.optimization_barrier((tie, scaled))
    scaled = lax.psum(scaled, "tp").astype(jnp.float32)
    first_mean = jnp.mean(scaled, axis=-1, keepdims=True)
    second_mean = jnp.mean(scaled * unit, axis=-1, keepdims=True)
    grad_input = grad_flat + inverse * (scaled - first_mean - unit * second_mean)
    small = jnp.concatenate(
        [norm_terms, grad_out_shift[None]], 0
    )
    grad_terms = (small, grad_qkv, grad_qkv_shift, grad_dense, grad_up, grad_up_shift, grad_down)
    return grad_input.reshape(seq_count, tok_rows, model_width), grad_terms, tie


SPLIT_AXES = (None, 2, None, 0, 1, None, 0)
CTX_AXES = (1, 0, 1, 1, 0, 0, 1)


def reduce_layer(terms, owner):
    section_index = lax.axis_index("section")
    ctx_count = lax.axis_size("ctx")
    context_index = lax.axis_index("ctx")
    small = terms[0]
    small = jnp.concatenate([lax.psum(small[:4], "tp"), small[4:]], 0)
    tiny = [small, terms[2], terms[5]]
    tiny_axes = [1, 1, 0]
    flat = []
    sizes = []
    for value, axis in zip(tiny, tiny_axes):
        moved = jnp.moveaxis(value, axis, 0)
        sizes.append(moved.shape)
        flat.append(moved.reshape(ctx_count, -1))
    packed = lax.psum(jnp.concatenate(flat, 1), ("section", "ctx"))
    packed = lax.dynamic_index_in_dim(packed, context_index, 0, keepdims=False)
    pieces = []
    offset = 0
    for shape, axis in zip(sizes, tiny_axes):
        width = math.prod(shape) // ctx_count
        piece = packed[offset : offset + width].reshape((shape[0] // ctx_count,) + shape[1:])
        pieces.append(jnp.moveaxis(piece, 0, axis))
        offset += width
    out = [pieces[0], None, pieces[1], None, None, pieces[2], None]
    for position in (1, 3, 4, 6):
        value = terms[position]
        split_axis = SPLIT_AXES[position]
        half = value.shape[split_axis] // 2
        mine = lax.dynamic_slice_in_dim(value, section_index * half, half, split_axis)
        theirs = lax.dynamic_slice_in_dim(value, (1 - section_index) * half, half, split_axis)
        summed = mine + swap_sections(theirs.astype(jnp.bfloat16)).astype(jnp.float32)
        reduced = lax.psum_scatter(
            summed.astype(jnp.bfloat16), "ctx", scatter_dimension=CTX_AXES[position], tiled=True
        ).astype(jnp.float32)
        moved = one_way(reduced, 1 - owner, owner)
        halves = [reduced, moved] if owner == 0 else [moved, reduced]
        out[position] = jnp.concatenate(halves, split_axis)
    return tuple(out)


def on_device(
    inputs,
    grad_out,
    ln1_gain,
    ln1_bias,
    ln2_gain,
    ln2_bias,
    w_qkv,
    qkv_bias,
    w_dense,
    w_up,
    up_bias,
    w_down,
    out_bias,
):
    section_index = lax.axis_index("section")
    context_index = lax.axis_index("ctx")
    ctx_count = lax.axis_size("ctx")
    micro_count, seq_count, tok_rows, model_width = inputs.shape
    seq_length = tok_rows * ctx_count
    head_dim = w_qkv.shape[3] // 3
    score_scale = 1.0 / math.sqrt(head_dim)

    own = gather_layer(ln1_gain, ln1_bias, ln2_gain, ln2_bias, w_qkv, qkv_bias, w_dense, w_up,
                       up_bias, w_down, out_bias)
    other = tuple(swap_sections(piece) for piece in own)
    first_layer = tuple(jnp.where(section_index == 0, a, b) for a, b in zip(own, other))
    second_layer = tuple(jnp.where(section_index == 0, b, a) for a, b in zip(own, other))

    query_index = context_index * tok_rows + jnp.arange(tok_rows, dtype=jnp.int32)
    allowed = jnp.arange(seq_length, dtype=jnp.int32)[None, :] <= query_index[:, None]
    cosine, sine = rotary_tables(query_index.astype(jnp.float32), head_dim // 4)

    rows = jnp.where(section_index == 0, inputs[0], inputs[1])
    grads = jnp.where(section_index == 0, grad_out[0], grad_out[1])

    mid, saved_first = layer_forward(rows, first_layer, cosine, sine, allowed, score_scale)
    top, saved_second = layer_forward(
        mid.astype(jnp.bfloat16), second_layer, cosine, sine, allowed, score_scale
    )
    grad_mid, terms_second, top = layer_backward(
        grads, saved_second, second_layer, cosine, sine, allowed, score_scale, top
    )
    top_other = one_way(top, 0, 1)
    reduced_second = reduce_layer(terms_second, 1)
    grad_in, terms_first, reduced_second = layer_backward(
        grad_mid, saved_first, first_layer, cosine, sine, allowed, score_scale, reduced_second
    )
    reduced_first = reduce_layer(terms_first, 0)
    grad_other = one_way(grad_in, 1, 0)
    small, g_qkv, g_qkv_shift, g_dense, g_up, g_up_shift, g_down = (
        jnp.where(section_index == 0, a, b) for a, b in zip(reduced_first, reduced_second)
    )

    block_ends = jnp.where(
        section_index == 0,
        jnp.stack([grad_in, grad_other]),
        jnp.stack([top_other, top]),
    )[None]
    return (
        block_ends,
        small[0][None],
        small[1][None],
        small[2][None],
        small[3][None],
        g_qkv[None],
        g_qkv_shift[None],
        g_dense[None],
        g_up[None],
        g_up_shift[None],
        g_down[None],
        small[4][None],
    )


def solution(mesh):
    placed = (
        P(None, None, "ctx", None),
        P(None, None, "ctx", None),
        P("section", "ctx"),
        P("section", "ctx"),
        P("section", "ctx"),
        P("section", "ctx"),
        P("section", "ctx", "tp", None),
        P("section", "tp", "ctx"),
        P("section", "tp", "ctx"),
        P("section", "ctx", "tp"),
        P("section", ("tp", "ctx")),
        P("section", "tp", "ctx"),
        P("section", "ctx"),
    )
    return jax.shard_map(
        on_device,
        mesh=mesh,
        in_specs=placed,
        out_specs=(
            P("section", None, None, "ctx", None),
            P("section", "ctx"),
            P("section", "ctx"),
            P("section", "ctx"),
            P("section", "ctx"),
            P("section", "ctx", "tp", None),
            P("section", "tp", "ctx"),
            P("section", "tp", "ctx"),
            P("section", "ctx", "tp"),
            P("section", ("tp", "ctx")),
            P("section", "tp", "ctx"),
            P("section", "ctx"),
        ),
        check_vma=False,
    )
```
